256 devices in a mesh: nodes: 64 (over z, x, core), fsdp: 4 (over y).
Axes of the slice: x: 4, y: 4, z: 8, core: 2. Of those that a mesh axis runs over, the one named last changes fastest.
Arguments:
- features: bfloat16 [512, 4, 128, 1024], P('nodes', 'fsdp'), may hold values from -6 to 6
- norm_gain: float32 [1024], replicated, may hold values from 0.25 to 1.75
- query_weight: bfloat16 [1024, 1024], P('fsdp'), may hold values from -1 to 1
- key_weight: bfloat16 [1024, 1024], P('fsdp'), may hold values from -1 to 1
- value_weight: bfloat16 [1024, 1024], P('fsdp'), may hold values from -0.1875 to 0.1875
- output_weight: bfloat16 [1024, 1024], P('fsdp'), may hold values from -0.1875 to 0.1875
- adjacency: int32 [512, 4, 8], P('nodes', 'fsdp'), may hold values from 0 to 511, as said below
- valid: int32 [512, 4, 8], P('nodes', 'fsdp'), may hold values 0 or 1
Outputs:
- updated: bfloat16 [512, 4, 128, 1024], P('nodes', 'fsdp')
The draws below stay inside these ranges and needn't reach their ends.
Inputs may be any that keep to these rules, and one draw needn't show every extreme that they name: adjacency[r, c, j] differs from r by 1 to 8; slots may repeat a cluster.
All inputs are finite; a program needn't handle non-finite values. No bound on the sum of `valid` on one device may be relied on, other than what follows from the above.
Results may differ from the reference program's by a relative error of at most 0.0047.
Values may be sent and summed in bfloat16 or wider, within the bound.
No kernel may reach another device: no remote copies, remote signals or barrier semaphores. Data moves between devices by JAX's collectives and lax.ppermute only.
A program may use at most 128 MiB of HBM per device.

```python
import jax
import jax.numpy as jnp
from jax import lax

D = 1024
HEADS = 16
HSIZE = 64
CSIZE = 128
NBR = 8
REACH = 8
ROWS = 512
COLS = 4


def draw_adjacency(key, part):
    first_key, second_key = jax.random.split(jax.random.fold_in(key, 11))
    shape = (ROWS, COLS, NBR)
    distance = jax.random.randint(first_key, shape, 1, REACH + 1)
    direction = 2 * jax.random.randint(second_key, shape, 0, 2) - 1
    own_row = lax.broadcasted_iota(jnp.int32, shape, 0)
    chosen = own_row + direction * distance
    inside = (chosen >= 0) & (chosen < ROWS)
    return jnp.where(inside, chosen, own_row - direction * distance).astype(jnp.int32)


def drawn_weight(key, salt):
    random_key = jax.random.fold_in(key, salt)
    return jax.random.truncated_normal(random_key, -4.0, 4.0, (D, D), jnp.float32) / D ** 0.5


def draw_query_weight(key, part):
    return drawn_weight(key, 21).astype(jnp.bfloat16)


def draw_key_weight(key, part):
    return drawn_weight(key, 22).astype(jnp.bfloat16)


def draw_features(key, part):
    base_key = jax.random.fold_in(jax.random.fold_in(key, 31), 0)
    array_shape = (ROWS, COLS, CSIZE, D)
    return jax.random.truncated_normal(base_key, -6.0, 6.0, array_shape, jnp.float32).astype(jnp.bfloat16)


def place_ends(result, own_key, smallest, high):
    longest = result.shape.index(max(result.shape))
    spots = []
    for shift in (0, 1):
        where = [jax.random.randint(jax.random.fold_in(own_key, axis), (), 0, length) for axis, length in enumerate(result.shape)]
        where[longest] = (where[longest] + shift) % result.shape[longest]
        spots.append(tuple(where))
    return result.at[spots[0]].set(smallest).at[spots[1]].set(high)


def levels(key, extent, cuts, smallest, high):
    gain = 1.0
    for dim, blocks in cuts:
        heights = jax.random.uniform(jax.random.fold_in(jax.random.fold_in(key, 6), dim), (blocks,), jnp.float32, smallest / len(cuts), high / len(cuts))
        gain = gain * jnp.repeat(jnp.exp(heights), extent[dim] // blocks).reshape((-1,) + (1,) * (len(extent) - 1 - dim))
    return gain


def gaussian(key, extent, deviation, bound, cuts=(), kind=jnp.bfloat16):
    result = deviation * jax.random.normal(key, extent, jnp.float32)
    if cuts:
        result = result * levels(key, extent, cuts, -0.22, 0.18)
    return jnp.clip(result, -bound, bound).astype(kind)


def setup_inputs(seed: int = 0) -> dict:
    splits = jax.random.split(jax.random.key(seed), 9)
    features = draw_features(jax.random.fold_in(splits[8], 71), 0)
    norm_gain = jnp.clip(1.0 + 0.15 * jax.random.normal(splits[1], (D,), jnp.float32), 0.25, 1.75)
    query_weight = draw_query_weight(jax.random.fold_in(splits[8], 71), 0)
    key_weight = draw_key_weight(jax.random.fold_in(splits[8], 71), 0)
    value_weight = gaussian(splits[4], (D, D), D ** -0.5, 0.1875, ((0, 4),))
    output_weight = gaussian(splits[5], (D, D), D ** -0.5, 0.1875, ((0, 4),))
    adjacency = draw_adjacency(jax.random.fold_in(splits[8], 71), 0)
    valid = place_ends((jax.random.randint(splits[7], (ROWS, COLS, NBR), 0, 4) < 3).astype(jnp.int32), jax.random.fold_in(splits[7], 1), 0, 1)
    return {"features": features, "norm_gain": norm_gain, "query_weight": query_weight, "key_weight": key_weight, "value_weight": value_weight, "output_weight": output_weight, "adjacency": adjacency, "valid": valid}


def attend(queries, key_rows, key_keep):
    count = queries.shape[0]
    model_width = queries.shape[1]
    query_heads = queries.reshape(count, HEADS, HSIZE).astype(jnp.float32)
    key_heads = key_rows[:, :model_width].reshape(-1, HEADS, HSIZE).astype(jnp.float32)
    value_heads = key_rows[:, model_width:].reshape(-1, HEADS, HSIZE).astype(jnp.float32)
    scores = jnp.einsum('qhd,khd->hqk', query_heads, key_heads) * (1.0 / HSIZE ** 0.5)
    scores = jnp.where(key_keep[None, None, :] > 0, scores, -1e+30)
    largest = lax.optimization_barrier(jnp.max(scores, axis=-1, keepdims=True))
    weights_exp = jnp.exp(scores - largest)
    denominator = lax.optimization_barrier(jnp.sum(weights_exp, axis=-1, keepdims=True))
    probs = (weights_exp / denominator).astype(jnp.bfloat16)
    context = jnp.einsum('hqk,khd->qhd', probs.astype(jnp.float32), value_heads)
    return context.reshape(count, model_width).astype(jnp.bfloat16)

def reference(features, norm_gain, query_weight, key_weight, value_weight, output_weight, adjacency, valid):
    row_count = features.shape[0]
    col_count = features.shape[1]
    flat = features.reshape(-1, D)
    wide = flat.astype(jnp.float32)
    mean_square = lax.optimization_barrier(jnp.mean(wide * wide, axis=-1, keepdims=True))
    normed = (wide * lax.rsqrt(mean_square + 1e-06) * norm_gain[None, :]).astype(jnp.bfloat16)
    queries = jnp.dot(normed, query_weight, preferred_element_type=jnp.float32).astype(jnp.bfloat16)
    keys = jnp.dot(normed, key_weight, preferred_element_type=jnp.float32).astype(jnp.bfloat16)
    values = jnp.dot(normed, value_weight, preferred_element_type=jnp.float32).astype(jnp.bfloat16)
    total = row_count * col_count
    key_value = jnp.concatenate([keys, values], axis=-1).reshape(total, CSIZE, 2 * D)
    query_blocks = queries.reshape(total, CSIZE, D)
    adjacency_flat = adjacency.reshape(total, NBR)
    valid_flat = valid.reshape(total, NBR)

    def one_cluster(packed):
        cluster, query_block, neighbor_rows, neighbor_valid = packed
        column = cluster % col_count
        neighbor_ids = (neighbor_rows * col_count + column).astype(jnp.int32)
        own = lax.dynamic_index_in_dim(key_value, cluster.astype(jnp.int32), 0, keepdims=True)
        others = jnp.take(key_value, neighbor_ids, axis=0)
        key_rows = jnp.concatenate([own, others], axis=0).reshape(-1, 2 * D)
        slot_keep = jnp.concatenate([jnp.ones((1,), jnp.int32), neighbor_valid.astype(jnp.int32)])
        key_keep = jnp.repeat(slot_keep, CSIZE)
        return attend(query_block, key_rows, key_keep)
    context = lax.map(one_cluster, (jnp.arange(total, dtype=jnp.int32), query_blocks, adjacency_flat, valid_flat))
    context = context.reshape(-1, D)
    projected = jnp.dot(context, output_weight, preferred_element_type=jnp.float32)
    updated = (wide + projected).astype(jnp.bfloat16)
    return updated.reshape(row_count, col_count, CSIZE, D)
```

```python
import functools

import jax
import jax.numpy as jnp
from jax import lax
from jax.experimental import pallas as pl
from jax.experimental.pallas import tpu as pltpu
from jax.sharding import Mesh
from jax.sharding import PartitionSpec as P

BF = jnp.bfloat16
F32 = jnp.float32
NODES = ("z", "x", "core")
HSIZE = 64
QSCALE = 1.4426950408889634 / HSIZE**0.5
ROWS = 8
CS = 128
D = 1024
TILE = 256
SHARD = 256


def swap_cores(t):
    return lax.ppermute(t, "core", [(0, 1), (1, 0)])


def gather_pieces(shards):
    up = [(i, (i + 1) % 4) for i in range(4)]
    down = [((i + 1) % 4, i) for i in range(4)]
    half = shards.shape[0] // 2
    a = lax.ppermute(shards, "fsdp", up)
    b = lax.ppermute(shards, "fsdp", down)
    c = lax.ppermute(a[:half], "fsdp", up)
    d = lax.ppermute(b[half:], "fsdp", down)
    return (a, b, c, d), tuple(swap_cores(t) for t in (a, b, c, d))


def half_rows(weight):
    core = lax.axis_index("core")
    return lax.dynamic_slice_in_dim(weight, core * (SHARD // 2), SHARD // 2, 0)


def place_halves(own, mine, other):
    y = lax.axis_index("fsdp")
    core = lax.axis_index("core")
    h = SHARD // 2
    pieces = [own]
    starts = [y * SHARD]
    for part, c in ((mine, core), (other, 1 - core)):
        a, b, e, f = part
        pieces += [a, b, e, f]
        starts += [
            (y + 3) % 4 * SHARD + c * h,
            (y + 1) % 4 * SHARD + c * h,
            (y + 2) % 4 * SHARD + c * h,
            (y + 2) % 4 * SHARD + c * h + h // 2,
        ]
    return pieces, starts


def project_kernel(starts, x_ref, gain_ref, *refs, count, per, scales, aliased):
    pieces = refs[: count * per]
    refs = refs[count * per + (count if aliased else 0) :]
    outs, (weights, sems) = refs[:count], refs[count:]
    step = pl.program_id(0)

    def copies():
        for w in range(count):
            for p in range(per):
                piece = pieces[w * per + p]
                rows = piece.shape[0]
                start = pl.multiple_of(starts[w * per + p], 64)
                yield pltpu.make_async_copy(
                    piece, weights.at[w, pl.ds(start, rows)], sems.at[w * per + p]
                )

    @pl.when(step == 0)
    def _():
        for c in copies():
            c.start()
        for c in copies():
            c.wait()

    wide = x_ref[...].astype(F32)
    mean = jnp.mean(wide * wide, axis=-1, keepdims=True)
    normed = (wide * lax.rsqrt(mean + 1e-06) * gain_ref[...]).astype(BF)
    for w in range(count):
        got = jnp.dot(normed, weights[w], preferred_element_type=F32)
        if scales[w] != 1.0:
            got = got * scales[w]
        outs[w][...] = got.astype(BF)


def project(name, x, gain, weights, scales, total, first, into=None):
    count = len(weights)
    per = len(weights[0][0])
    pieces = [p for w in weights for p in w[0]]
    starts = jnp.stack([jnp.asarray(s, jnp.int32) for w in weights for s in w[1]])
    rows = x.shape[0]
    hbm = pl.BlockSpec(memory_space=pl.ANY)
    extra = list(into) if into is not None else []
    kernel = functools.partial(
        project_kernel, count=count, per=per, scales=scales, aliased=bool(extra)
    )
    return pl.pallas_call(
        kernel,
        out_shape=[jax.ShapeDtypeStruct((total, D), BF)] * count,
        grid_spec=pltpu.PrefetchScalarGridSpec(
            num_scalar_prefetch=1,
            grid=(rows // TILE,),
            in_specs=[
                pl.BlockSpec((TILE, D), lambda i, s: (i, 0)),
                pl.BlockSpec((1, D), lambda i, s: (0, 0)),
            ]
            + [hbm] * (len(pieces) + len(extra)),
            out_specs=[pl.BlockSpec((TILE, D), lambda i, s: (i + first // TILE, 0))]
            * count,
            scratch_shapes=[
                pltpu.VMEM((count, D, D), BF),
                pltpu.SemaphoreType.DMA((len(pieces),)),
            ],
        ),
        input_output_aliases={3 + len(pieces) + i: i for i in range(len(extra))},
        compiler_params=pltpu.CompilerParams(vmem_limit_bytes=40 << 20),
        cost_estimate=pl.CostEstimate(
            flops=2 * rows * D * D * count,
            bytes_accessed=2 * (rows * D * (1 + count) + count * D * D),
            transcendentals=0,
        ),
        name=name,
    )(starts, x, gain, *pieces, *extra)


def attend_kernel(
    slots, counts, starts, q_ref, k_ref, v_ref, f_ref, *refs, n_pieces
):
    pieces = refs[:n_pieces]
    o_ref, ctx, acc, weight, sems = refs[n_pieces:]
    group = pl.program_id(0)
    last = pl.num_programs(0) - 1

    def copies():
        for p in range(n_pieces):
            start = pl.multiple_of(starts[p], 64)
            yield pltpu.make_async_copy(
                pieces[p], weight.at[pl.ds(start, pieces[p].shape[0])], sems.at[p]
            )

    @pl.when(group == 0)
    def _():
        for c in copies():
            c.start()

    def cluster(r, carry):
        def variant(blocks):
            def run():
                q = q_ref[r]
                head = lax.broadcasted_iota(jnp.int32, (CS, 4 * HSIZE), 1) // HSIZE
                stacked = jnp.concatenate(
                    [jnp.where(head == h, q, jnp.zeros_like(q)) for h in range(4)], 0
                )
                ids = [slots[r, j] for j in range(blocks)]
                scores = []
                for j in range(0, blocks, 2):
                    keys = jnp.concatenate([k_ref[i] for i in ids[j : j + 2]], 0)
                    scores.append(
                        lax.dot_general(
                            stacked,
                            keys,
                            (((1,), (1,)), ((), ())),
                            preferred_element_type=F32,
                        )
                    )
                top = None
                for s in scores:
                    for t in range(0, s.shape[1], 128):
                        part = s[:, t : t + 128]
                        top = part if top is None else jnp.maximum(top, part)
                top = jnp.max(top, axis=1, keepdims=True)
                probs = [jnp.exp2(s - top).astype(BF) for s in scores]
                left = lax.broadcasted_iota(jnp.int32, (CS, 128), 1) < HSIZE
                for t in range(2):
                    lanes = slice(128 * t, 128 * t + 128)
                    total = None
                    for n, j in enumerate(range(0, blocks, 2)):
                        vals = jnp.concatenate(
                            [v_ref[i, :, lanes] for i in ids[j : j + 2]], 0
                        )
                        both = jnp.concatenate([vals, jnp.ones(vals.shape, BF)], 1)
                        d = jnp.dot(
                            probs[n][256 * t : 256 * t + 256],
                            both,
                            preferred_element_type=F32,
                        )
                        total = d if total is None else total + d
                    c = total[:, :128] / total[:, 128:]
                    ctx[r, :, lanes] = jnp.where(left, c[:CS], c[CS:]).astype(BF)

            return run

        lax.switch(counts[r] - 1, [variant(n) for n in range(1, 10)])
        return carry

    lax.fori_loop(0, ROWS, cluster, 0)

    @pl.when(group == 0)
    def _():
        for c in copies():
            c.wait()

    rows = pl.ds(pl.multiple_of(group * 256, 256), 256)
    part = jnp.dot(
        ctx[...].reshape(ROWS * CS, 256), weight[rows], preferred_element_type=F32
    )

    @pl.when(group == 0)
    def _():
        acc[...] = part

    @pl.when(jnp.logical_and(group > 0, group < last))
    def _():
        acc[...] += part

    @pl.when(group == last)
    def _():
        o_ref[...] = (f_ref[...].astype(F32) + acc[...] + part).astype(BF)


def attend(slots, counts, queries, keys, values, features, weight):
    pieces, starts = weight
    starts = jnp.stack([jnp.asarray(s, jnp.int32) for s in starts])
    n = len(pieces)
    return pl.pallas_call(
        functools.partial(attend_kernel, n_pieces=n),
        out_shape=jax.ShapeDtypeStruct((ROWS * CS, D), BF),
        grid_spec=pltpu.PrefetchScalarGridSpec(
            num_scalar_prefetch=3,
            grid=(4,),
            in_specs=[
                pl.BlockSpec((ROWS, CS, 256), lambda g, *_: (0, 0, g)),
                pl.BlockSpec((3 * ROWS, CS, 256), lambda g, *_: (0, 0, g)),
                pl.BlockSpec((3 * ROWS, CS, 256), lambda g, *_: (0, 0, g)),
                pl.BlockSpec((ROWS * CS, D), lambda g, *_: (0, 0)),
            ]
            + [pl.BlockSpec(memory_space=pl.ANY)] * n,
            out_specs=pl.BlockSpec((ROWS * CS, D), lambda g, *_: (0, 0)),
            scratch_shapes=[
                pltpu.VMEM((ROWS, CS, 256), BF),
                pltpu.VMEM((ROWS * CS, D), F32),
                pltpu.VMEM((D, D), BF),
                pltpu.SemaphoreType.DMA((n,)),
            ],
        ),
        compiler_params=pltpu.CompilerParams(vmem_limit_bytes=60 << 20),
        cost_estimate=pl.CostEstimate(
            flops=20 << 30, bytes_accessed=20 << 20, transcendentals=0
        ),
        name="attend",
    )(slots, counts, starts, queries, keys, values, features, *pieces)


def key_slots(adjacency, valid, node):
    index = adjacency[:, 0, :] - node * ROWS + ROWS
    used = (valid[:, 0, :] > 0).astype(jnp.int32)
    before = jnp.sum(
        used[:, None, :] * (jnp.arange(8)[None, :, None] > jnp.arange(8)[None, None, :]), -1
    )
    hit = used[:, :, None] * (before[:, :, None] == jnp.arange(8)[None, None, :])
    listed = jnp.sum(index[:, :, None] * hit, 1)
    own = (jnp.arange(ROWS, dtype=jnp.int32) + ROWS)[:, None]
    return jnp.concatenate([own, listed], 1).astype(jnp.int32), (
        1 + jnp.sum(used, 1)
    ).astype(jnp.int32)


def per_device(
    features, norm_gain, query_weight, key_weight, value_weight, output_weight, adjacency, valid
):
    flat = features.reshape(ROWS * CS, D)
    n = lax.axis_size("z") * lax.axis_size("x") * 2
    above = lax.ppermute(flat, NODES, [(i, i + 1) for i in range(n - 1)])
    below = lax.ppermute(flat, NODES, [(i + 1, i) for i in range(n - 1)])
    gathered = []
    for weight in (key_weight, value_weight, query_weight, output_weight):
        mine, other = gather_pieces(half_rows(weight))
        gathered.append(place_halves(weight, mine, other))
    wk, wv, wq, wo = gathered
    gain = norm_gain.reshape(1, D)
    node = lax.axis_index(NODES)
    slots, counts = key_slots(adjacency, valid, node)
    own = ROWS * CS
    kv = project("own_kv", flat, gain, [wk, wv], (1.0, 1.0), 3 * own, own)
    (queries,) = project("own_q", flat, gain, [wq], (QSCALE,), own, 0)
    kv = project("above_kv", above, gain, [wk, wv], (1.0, 1.0), 3 * own, 0, kv)
    keys, values = project("below_kv", below, gain, [wk, wv], (1.0, 1.0), 3 * own, 2 * own, kv)
    window = (3 * ROWS, CS, D)
    out = attend(
        slots,
        counts,
        queries.reshape(ROWS, CS, D),
        keys.reshape(window),
        values.reshape(window),
        flat,
        wo,
    )
    return out.reshape(ROWS, 1, CS, D)


def solution(mesh):
    nodes, fsdp = mesh.devices.shape
    split = Mesh(mesh.devices.reshape(nodes // 8, 4, 2, fsdp), NODES + ("fsdp",))
    in_specs = (
        P(NODES, "fsdp", None, None),
        P(),
        P("fsdp", None),
        P("fsdp", None),
        P("fsdp", None),
        P("fsdp", None),
        P(NODES, "fsdp", None),
        P(NODES, "fsdp", None),
    )
    out_specs = P(NODES, "fsdp", None, None)
    return jax.shard_map(
        per_device, mesh=split, in_specs=in_specs, out_specs=out_specs, check_vma=False
    )
```

```python
import functools

import jax
import jax.numpy as jnp
from jax import lax
from jax.experimental import pallas as pl
from jax.experimental.pallas import tpu as pltpu
from jax.sharding import Mesh
from jax.sharding import PartitionSpec as P

BF = jnp.bfloat16
F32 = jnp.float32
NODES = ("z", "x", "core")
HSIZE = 64
QSCALE = 1.4426950408889634 / HSIZE**0.5
ROWS = 8
CS = 128
D = 1024
TILE = 256
SHARD = 256
WIDE = 512


def swap_cores(t):
    return lax.ppermute(t, "core", [(0, 1), (1, 0)])


def split_kernel(core, k_ref, v_ref, q_ref, o_ref, first, second):
    half = SHARD // 2
    for i, ref in enumerate((k_ref, v_ref, q_ref)):
        first[i * half : (i + 1) * half] = ref[...]
    second[...] = o_ref[...]


def split_rows(weights, core):
    half = SHARD // 2
    return pl.pallas_call(
        split_kernel,
        out_shape=[
            jax.ShapeDtypeStruct((3 * half, D), BF),
            jax.ShapeDtypeStruct((half, D), BF),
        ],
        grid_spec=pltpu.PrefetchScalarGridSpec(
            num_scalar_prefetch=1,
            grid=(1,),
            in_specs=[pl.BlockSpec((half, D), lambda i, c: (c[0], 0))] * 4,
            out_specs=[
                pl.BlockSpec((3 * half, D), lambda i, c: (0, 0)),
                pl.BlockSpec((half, D), lambda i, c: (0, 0)),
            ],
        ),
        name="split_rows",
    )(core.reshape(1), *weights)


UP = [(i, (i + 1) % 4) for i in range(4)]
DOWN = [((i + 1) % 4, i) for i in range(4)]


def relayed_rows(part, after):
    half = part.shape[0] // 2
    below = lax.ppermute(part, "fsdp", UP)
    above = lax.ppermute(part, "fsdp", DOWN)
    below, above, after = lax.optimization_barrier((below, above, after))
    far = (
        lax.ppermute(below[:half], "fsdp", UP),
        lax.ppermute(above[half:], "fsdp", DOWN),
    )
    mine = (below, above) + far
    return mine + tuple(swap_cores(t) for t in mine), after


def direct_rows(part):
    return [
        lax.ppermute(part, "fsdp", [(i, (i + k) % 4) for i in range(4)]) for k in (1, 3, 2)
    ]


def piece_plan(index, count):
    h = SHARD // 2
    if count == 1:
        return [(i, 0, h, i + 1, 0) for i in range(6)]
    total = count * h
    plan = []
    for side in range(2):
        plan.append((4 * side, index * h, h, 1 + 3 * side, 0))
        plan.append((4 * side + 1, index * h, h, 2 + 3 * side, 0))
        for part, (lo, hi) in enumerate(((0, total // 2), (total // 2, total))):
            first = max(lo, index * h)
            last = min(hi, (index + 1) * h)
            if first < last:
                plan.append(
                    (4 * side + 2 + part, first - lo, last - first, 3 + 3 * side, first - index * h)
                )
    return plan


def place_starts(y, core):
    h = SHARD // 2
    starts = [y * SHARD]
    for side in (core, 1 - core):
        starts += [(y + k) % 4 * SHARD + side * h for k in (3, 1, 2)]
    return jnp.stack(starts).astype(jnp.int32)


def weight_copies(starts, shard, arrays, index, count, target, sems):
    row = pl.multiple_of(starts[0], SHARD)
    copies = [pltpu.make_async_copy(shard, target.at[pl.ds(row, SHARD)], sems.at[0])]
    for n, (array, first, rows, place, offset) in enumerate(piece_plan(index, count)):
        row = pl.multiple_of(starts[place] + offset, 64)
        copies.append(
            pltpu.make_async_copy(
                arrays[array].at[pl.ds(first, rows)],
                target.at[pl.ds(row, rows)],
                sems.at[n + 1],
            )
        )
    return copies


PIECES = 9


def project_kernel(starts, x_ref, gain_ref, *refs, count, stacked, scales):
    shards, arrays, refs = refs[:count], refs[count : count + 8], refs[count + 8 :]
    outs, (weights, sems) = refs[:count], refs[count:]
    step = pl.program_id(0)

    def copies(w):
        return weight_copies(starts, shards[w], arrays, w, stacked, weights.at[w], sems.at[w])

    @pl.when(step == 0)
    def _():
        for w in range(count):
            for c in copies(w):
                c.start()

    wide = x_ref[...].astype(F32)
    mean = jnp.mean(wide * wide, axis=-1, keepdims=True)
    normed = (wide * lax.rsqrt(mean + 1e-06) * gain_ref[...]).astype(BF)
    for w in range(count):

        @pl.when(step == 0)
        def _():
            for c in copies(w):
                c.wait()

        got = jnp.dot(normed, weights[w], preferred_element_type=F32)
        if scales[w] != 1.0:
            got = got * scales[w]
        outs[w][...] = got.astype(BF)


def project(name, x, gain, starts, shards, arrays, stacked, scales):
    count = len(shards)
    rows = x.shape[0]
    return pl.pallas_call(
        functools.partial(project_kernel, count=count, stacked=stacked, scales=scales),
        out_shape=[jax.ShapeDtypeStruct((rows, D), BF)] * count,
        grid_spec=pltpu.PrefetchScalarGridSpec(
            num_scalar_prefetch=1,
            grid=(rows // TILE,),
            in_specs=[
                pl.BlockSpec((TILE, D), lambda i, s: (i, 0)),
                pl.BlockSpec((1, D), lambda i, s: (0, 0)),
            ]
            + [pl.BlockSpec(memory_space=pltpu.HBM)] * (count + 8),
            out_specs=[pl.BlockSpec((TILE, D), lambda i, s: (i, 0))] * count,
            scratch_shapes=[
                pltpu.VMEM((count, D, D), BF),
                pltpu.SemaphoreType.DMA((count, PIECES)),
            ],
        ),
        compiler_params=pltpu.CompilerParams(vmem_limit_bytes=56 << 20),
        cost_estimate=pl.CostEstimate(
            flops=2 * rows * D * D * count * 16,
            bytes_accessed=2 * (rows * D * (1 + count) + count * D * D),
            transcendentals=0,
        ),
        name=name,
    )(starts, x, gain, *shards, *arrays)


def attend_kernel(slots, counts, starts, q_ref, f_ref, *refs):
    key_refs, value_refs, refs = refs[:3], refs[3:6], refs[6:]
    shard, arrays, refs = refs[0], refs[1:7], refs[7:]
    o_ref, keys, values, ctx, acc, weight, weight_sems, sems = refs
    group = pl.program_id(0)
    groups = pl.num_programs(0)

    def output_copies():
        return weight_copies(starts, shard, arrays, 0, 1, weight, weight_sems)

    def window_copies(g):
        lanes = pl.ds(pl.multiple_of(g * WIDE, WIDE), WIDE)
        for n, (sources, target) in enumerate(((key_refs, keys), (value_refs, values))):
            for p in range(3):
                yield pltpu.make_async_copy(
                    sources[p].at[:, :, lanes],
                    target.at[g, pl.ds(p * ROWS, ROWS)],
                    sems.at[g, 3 * n + p],
                )

    @pl.when(group == 0)
    def _():
        for g in range(D // WIDE):
            for c in window_copies(g):
                c.start()
        for c in output_copies():
            c.start()

    for c in window_copies(group):
        c.wait()

    def cluster(r, carry):
        def variant(blocks):
            def run():
                head = lax.broadcasted_iota(jnp.int32, (CS, 128), 1) // HSIZE
                left = head == 0
                ids = [slots[r, j] for j in range(blocks)]
                for t in range(WIDE // 128):
                    lanes = slice(128 * t, 128 * t + 128)
                    q = q_ref[r, :, lanes]
                    stacked = jnp.concatenate(
                        [jnp.where(head == h, q, jnp.zeros_like(q)) for h in range(2)], 0
                    )
                    scores = []
                    for j in range(0, blocks, 2):
                        block = jnp.concatenate(
                            [keys[group, i, :, lanes] for i in ids[j : j + 2]], 0
                        )
                        scores.append(
                            lax.dot_general(
                                stacked,
                                block,
                                (((1,), (1,)), ((), ())),
                                preferred_element_type=F32,
                            )
                        )
                    top = None
                    for s in scores:
                        for u in range(0, s.shape[1], 128):
                            part = s[:, u : u + 128]
                            top = part if top is None else jnp.maximum(top, part)
                    top = jnp.max(top, axis=1, keepdims=True)
                    total = None
                    for n, j in enumerate(range(0, blocks, 2)):
                        probs = jnp.exp2(scores[n] - top).astype(BF)
                        vals = jnp.concatenate(
                            [values[group, i, :, lanes] for i in ids[j : j + 2]], 0
                        )
                        both = jnp.concatenate([vals, jnp.ones(vals.shape, BF)], 1)
                        d = jnp.dot(probs, both, preferred_element_type=F32)
                        total = d if total is None else total + d
                    num = jnp.where(left, total[:CS, :128], total[CS:, :128])
                    den = jnp.where(left, total[:CS, 128:], total[CS:, 128:])
                    ctx[r, :, lanes] = (num / den).astype(BF)

            return run

        lax.switch(counts[r] - 1, [variant(n) for n in range(1, 10)])
        return carry

    lax.fori_loop(0, ROWS, cluster, 0)

    @pl.when(group == 0)
    def _():
        for c in output_copies():
            c.wait()

    rows = pl.ds(pl.multiple_of(group * WIDE, WIDE), WIDE)
    part = jnp.dot(
        ctx[...].reshape(ROWS * CS, WIDE), weight[rows], preferred_element_type=F32
    )

    @pl.when(group == 0)
    def _():
        acc[...] = part

    @pl.when(jnp.logical_and(group > 0, group < groups - 1))
    def _():
        acc[...] += part

    @pl.when(group == groups - 1)
    def _():
        o_ref[...] = (f_ref[...].astype(F32) + acc[...] + part).astype(BF)


def attend(slots, counts, starts, queries, keys, values, features, shard, arrays):
    hbm = pl.BlockSpec(memory_space=pltpu.HBM)
    window = (D // WIDE, 3 * ROWS, CS, WIDE)
    return pl.pallas_call(
        attend_kernel,
        out_shape=jax.ShapeDtypeStruct((ROWS * CS, D), BF),
        grid_spec=pltpu.PrefetchScalarGridSpec(
            num_scalar_prefetch=3,
            grid=(D // WIDE,),
            in_specs=[
                pl.BlockSpec((ROWS, CS, WIDE), lambda g, *_: (0, 0, g)),
                pl.BlockSpec((ROWS * CS, D), lambda g, *_: (0, 0)),
            ]
            + [hbm] * (6 + 7),
            out_specs=pl.BlockSpec((ROWS * CS, D), lambda g, *_: (0, 0)),
            scratch_shapes=[
                pltpu.VMEM(window, BF),
                pltpu.VMEM(window, BF),
                pltpu.VMEM((ROWS, CS, WIDE), BF),
                pltpu.VMEM((ROWS * CS, D), F32),
                pltpu.VMEM((D, D), BF),
                pltpu.SemaphoreType.DMA((PIECES,)),
                pltpu.SemaphoreType.DMA((D // WIDE, 6)),
            ],
        ),
        compiler_params=pltpu.CompilerParams(vmem_limit_bytes=60 << 20),
        cost_estimate=pl.CostEstimate(
            flops=30 << 30, bytes_accessed=20 << 20, transcendentals=0
        ),
        name="attend",
    )(slots, counts, starts, queries, features, *keys, *values, shard, *arrays)


def key_slots(adjacency, valid, node, core):
    row = adjacency[:, 0, :] - node * ROWS
    low = jnp.where(core == 0, 3 * ROWS, 2 * ROWS)
    high = jnp.where(core == 0, 0, ROWS)
    index = row + jnp.where(row < 0, low, jnp.where(row >= ROWS, high, 0))
    used = (valid[:, 0, :] > 0).astype(jnp.int32)
    before = jnp.sum(
        used[:, None, :] * (jnp.arange(8)[None, :, None] > jnp.arange(8)[None, None, :]), -1
    )
    hit = used[:, :, None] * (before[:, :, None] == jnp.arange(8)[None, None, :])
    listed = jnp.sum(index[:, :, None] * hit, 1)
    own = jnp.arange(ROWS, dtype=jnp.int32)[:, None]
    return jnp.concatenate([own, listed], 1).astype(jnp.int32), (
        1 + jnp.sum(used, 1)
    ).astype(jnp.int32)


def per_device(
    features, norm_gain, query_weight, key_weight, value_weight, output_weight, adjacency, valid
):
    flat = features.reshape(ROWS * CS, D)
    n = lax.axis_size("z") * lax.axis_size("x") * 2
    pairs = [(i, i + 1) for i in range(1, n - 1, 2)]
    off = lax.ppermute(flat, NODES, pairs + [(j, i) for i, j in pairs])
    core = lax.axis_index("core")
    shards = (key_weight, value_weight, query_weight)
    part, output_part = split_rows(shards + (output_weight,), core)
    tables = (
        *key_slots(adjacency, valid, lax.axis_index(NODES), core),
        place_starts(lax.axis_index("fsdp"), core),
    )
    arrays, (slots, counts, starts) = relayed_rows(part, tables)
    output_part, _ = lax.optimization_barrier((output_part, arrays[2:4]))
    output_arrays = direct_rows(output_part)
    gain = norm_gain.reshape(1, D)
    mine, off = lax.optimization_barrier((flat, off))
    keys, values, queries = project(
        "own", mine, gain, starts, shards, arrays, 3, (1.0, 1.0, QSCALE)
    )
    near_keys, near_values = swap_cores(keys), swap_cores(values)
    queries, *output_arrays = lax.optimization_barrier((queries, *output_arrays))
    output_arrays += [swap_cores(t) for t in output_arrays]
    off_keys, off_values = project("off", off, gain, starts, shards[:2], arrays, 3, (1.0, 1.0))

    def cells(t):
        return t.reshape(ROWS, CS, D)

    out = attend(
        slots,
        counts,
        starts,
        cells(queries),
        [cells(t) for t in (keys, near_keys, off_keys)],
        [cells(t) for t in (values, near_values, off_values)],
        mine,
        output_weight,
        output_arrays,
    )
    return out.reshape(ROWS, 1, CS, D)


def solution(mesh):
    nodes, fsdp = mesh.devices.shape
    split = Mesh(mesh.devices.reshape(nodes // 8, 4, 2, fsdp), NODES + ("fsdp",))
    in_specs = (
        P(NODES, "fsdp", None, None),
        P(),
        P("fsdp", None),
        P("fsdp", None),
        P("fsdp", None),
        P("fsdp", None),
        P(NODES, "fsdp", None),
        P(NODES, "fsdp", None),
    )
    out_specs = P(NODES, "fsdp", None, None)
    return jax.shard_map(
        per_device, mesh=split, in_specs=in_specs, out_specs=out_specs, check_vma=False
    )
```

```python
import functools

import jax
import jax.numpy as jnp
from jax import lax
from jax.experimental import pallas as pl
from jax.experimental.pallas import tpu as pltpu
from jax.sharding import Mesh
from jax.sharding import PartitionSpec as P

BF = jnp.bfloat16
F32 = jnp.float32
NODES = ("z", "x", "core")
HSIZE = 64
QSCALE = 1.4426950408889634 / HSIZE**0.5
ROWS = 8
CS = 128
D = 1024
TILE = 256
SHARD = 256
WIDE = 512
SAFE = 9000.0


def swap_cores(t):
    return lax.ppermute(t, "core", [(0, 1), (1, 0)])


def split_kernel(core, k_ref, v_ref, q_ref, o_ref, first, second):
    half = SHARD // 2
    for i, ref in enumerate((k_ref, v_ref, q_ref)):
        first[i * half : (i + 1) * half] = ref[...]
    second[...] = o_ref[...]


def split_rows(weights, core):
    half = SHARD // 2
    return pl.pallas_call(
        split_kernel,
        out_shape=[
            jax.ShapeDtypeStruct((3 * half, D), BF),
            jax.ShapeDtypeStruct((half, D), BF),
        ],
        grid_spec=pltpu.PrefetchScalarGridSpec(
            num_scalar_prefetch=1,
            grid=(1,),
            in_specs=[pl.BlockSpec((half, D), lambda i, c: (c[0], 0))] * 4,
            out_specs=[
                pl.BlockSpec((3 * half, D), lambda i, c: (0, 0)),
                pl.BlockSpec((half, D), lambda i, c: (0, 0)),
            ],
        ),
        name="split_rows",
    )(core.reshape(1), *weights)


UP = [(i, (i + 1) % 4) for i in range(4)]
DOWN = [((i + 1) % 4, i) for i in range(4)]


def relayed_rows(part, after):
    half = part.shape[0] // 2
    below = lax.ppermute(part, "fsdp", UP)
    above = lax.ppermute(part, "fsdp", DOWN)
    below, above, after = lax.optimization_barrier((below, above, after))
    far = (
        lax.ppermute(below[:half], "fsdp", UP),
        lax.ppermute(above[half:], "fsdp", DOWN),
    )
    mine = (below, above) + far
    return mine + tuple(swap_cores(t) for t in mine), after


def direct_rows(part):
    return [
        lax.ppermute(part, "fsdp", [(i, (i + k) % 4) for i in range(4)]) for k in (1, 3, 2)
    ]


def piece_plan(index, count):
    h = SHARD // 2
    if count == 1:
        return [(i, 0, h, i + 1, 0) for i in range(6)]
    total = count * h
    plan = []
    for side in range(2):
        plan.append((4 * side, index * h, h, 1 + 3 * side, 0))
        plan.append((4 * side + 1, index * h, h, 2 + 3 * side, 0))
        for part, (lo, hi) in enumerate(((0, total // 2), (total // 2, total))):
            first = max(lo, index * h)
            last = min(hi, (index + 1) * h)
            if first < last:
                plan.append(
                    (4 * side + 2 + part, first - lo, last - first, 3 + 3 * side, first - index * h)
                )
    return plan


def place_starts(y, core):
    h = SHARD // 2
    starts = [y * SHARD]
    for side in (core, 1 - core):
        starts += [(y + k) % 4 * SHARD + side * h for k in (3, 1, 2)]
    return jnp.stack(starts).astype(jnp.int32)


def weight_copies(starts, shard, arrays, index, count, target, sems):
    row = pl.multiple_of(starts[0], SHARD)
    copies = [pltpu.make_async_copy(shard, target.at[pl.ds(row, SHARD)], sems.at[0])]
    for n, (array, first, rows, place, offset) in enumerate(piece_plan(index, count)):
        row = pl.multiple_of(starts[place] + offset, 64)
        copies.append(
            pltpu.make_async_copy(
                arrays[array].at[pl.ds(first, rows)],
                target.at[pl.ds(row, rows)],
                sems.at[n + 1],
            )
        )
    return copies


PIECES = 9


def head_squares(t):
    wide = D // 2
    squares = t[:, :wide] * t[:, :wide] + t[:, wide:] * t[:, wide:]
    lane = lax.broadcasted_iota(jnp.int32, (wide, 128), 1)
    feature = lax.broadcasted_iota(jnp.int32, (wide, 128), 0)
    pick = (feature // HSIZE == lane).astype(BF)
    sums = jnp.dot(squares.astype(BF), pick, preferred_element_type=F32)
    return jnp.broadcast_to(jnp.max(sums, axis=0, keepdims=True), (8, 128))


def project_kernel(starts, x_ref, gain_ref, *refs, count, stacked, scales, squared):
    shards, arrays, refs = refs[:count], refs[count : count + 8], refs[count + 8 :]
    outs, squares, (weights, sems) = refs[:count], refs[count:-2], refs[-2:]
    step = pl.program_id(0)

    def copies(w):
        return weight_copies(starts, shards[w], arrays, w, stacked, weights.at[w], sems.at[w])

    @pl.when(step == 0)
    def _():
        for w in range(count):
            for c in copies(w):
                c.start()
        for ref in squares:
            ref[...] = jnp.zeros_like(ref)

    wide = x_ref[...].astype(F32)
    mean = jnp.mean(wide * wide, axis=-1, keepdims=True)
    normed = (wide * lax.rsqrt(mean + 1e-06) * gain_ref[...]).astype(BF)
    for w in range(count):

        @pl.when(step == 0)
        def _():
            for c in copies(w):
                c.wait()

        got = jnp.dot(normed, weights[w], preferred_element_type=F32)
        if scales[w] != 1.0:
            got = got * scales[w]
        if w in squared:
            ref = squares[squared.index(w)]
            ref[...] = jnp.maximum(ref[...], head_squares(got))
        outs[w][...] = got.astype(BF)


def project(name, x, gain, starts, shards, arrays, stacked, scales, squared):
    count = len(shards)
    rows = x.shape[0]
    return pl.pallas_call(
        functools.partial(
            project_kernel, count=count, stacked=stacked, scales=scales, squared=squared
        ),
        out_shape=[jax.ShapeDtypeStruct((rows, D), BF)] * count
        + [jax.ShapeDtypeStruct((8, 128), F32)] * len(squared),
        grid_spec=pltpu.PrefetchScalarGridSpec(
            num_scalar_prefetch=1,
            grid=(rows // TILE,),
            in_specs=[
                pl.BlockSpec((TILE, D), lambda i, s: (i, 0)),
                pl.BlockSpec((1, D), lambda i, s: (0, 0)),
            ]
            + [pl.BlockSpec(memory_space=pltpu.HBM)] * (count + 8),
            out_specs=[pl.BlockSpec((TILE, D), lambda i, s: (i, 0))] * count
            + [pl.BlockSpec((8, 128), lambda i, s: (0, 0))] * len(squared),
            scratch_shapes=[
                pltpu.VMEM((count, D, D), BF),
                pltpu.SemaphoreType.DMA((count, PIECES)),
            ],
        ),
        compiler_params=pltpu.CompilerParams(vmem_limit_bytes=56 << 20),
        cost_estimate=pl.CostEstimate(
            flops=2 * rows * D * D * count * 16,
            bytes_accessed=2 * (rows * D * (1 + count) + count * D * D),
            transcendentals=0,
        ),
        name=name,
    )(starts, x, gain, *shards, *arrays)


def attend_kernel(slots, counts, starts, q_ref, f_ref, *refs):
    square_refs, refs = refs[:4], refs[4:]
    key_refs, value_refs, refs = refs[:3], refs[3:6], refs[6:]
    shard, arrays, refs = refs[0], refs[1:7], refs[7:]
    o_ref, keys, values, ctx, acc, weight, weight_sems, sems = refs
    group = pl.program_id(0)
    groups = pl.num_programs(0)

    def output_copies():
        return weight_copies(starts, shard, arrays, 0, 1, weight, weight_sems)

    def window_copies(g):
        lanes = pl.ds(pl.multiple_of(g * WIDE, WIDE), WIDE)
        for n, (sources, target) in enumerate(((key_refs, keys), (value_refs, values))):
            for p in range(3):
                yield pltpu.make_async_copy(
                    sources[p].at[:, :, lanes],
                    target.at[g, pl.ds(p * ROWS, ROWS)],
                    sems.at[g, 3 * n + p],
                )

    @pl.when(group == 0)
    def _():
        for g in range(D // WIDE):
            for c in window_copies(g):
                c.start()
        for c in output_copies():
            c.start()

    for c in window_copies(group):
        c.wait()

    key_squares = jnp.maximum(
        jnp.maximum(square_refs[0][...], square_refs[1][...]), square_refs[2][...]
    )
    shifted = jnp.where(jnp.max(key_squares * square_refs[3][...]) < SAFE, 0, 9)

    def cluster(r, carry):
        def variant(blocks, shift):
            def run():
                head = lax.broadcasted_iota(jnp.int32, (CS, 128), 1) // HSIZE
                left = head == 0
                ids = [slots[r, j] for j in range(blocks)]
                for t in range(WIDE // 128):
                    lanes = slice(128 * t, 128 * t + 128)
                    q = q_ref[r, :, lanes]
                    stacked = jnp.concatenate(
                        [jnp.where(head == h, q, jnp.zeros_like(q)) for h in range(2)], 0
                    )
                    scores = []
                    for j in range(0, blocks, 2):
                        block = jnp.concatenate(
                            [keys[group, i, :, lanes] for i in ids[j : j + 2]], 0
                        )
                        scores.append(
                            lax.dot_general(
                                stacked,
                                block,
                                (((1,), (1,)), ((), ())),
                                preferred_element_type=F32,
                            )
                        )
                    if shift:
                        top = None
                        for s in scores:
                            for u in range(0, s.shape[1], 128):
                                part = s[:, u : u + 128]
                                top = part if top is None else jnp.maximum(top, part)
                        top = jnp.max(top, axis=1, keepdims=True)
                        scores = [s - top for s in scores]
                    total = None
                    for n, j in enumerate(range(0, blocks, 2)):
                        probs = jnp.exp2(scores[n]).astype(BF)
                        vals = jnp.concatenate(
                            [values[group, i, :, lanes] for i in ids[j : j + 2]], 0
                        )
                        both = jnp.concatenate([vals, jnp.ones(vals.shape, BF)], 1)
                        d = jnp.dot(probs, both, preferred_element_type=F32)
                        total = d if total is None else total + d
                    num = jnp.where(left, total[:CS, :128], total[CS:, :128])
                    den = jnp.where(left, total[:CS, 128:], total[CS:, 128:])
                    ctx[r, :, lanes] = (num / den).astype(BF)

            return run

        lax.switch(
            counts[r] - 1 + shifted,
            [variant(n, shift) for shift in (False, True) for n in range(1, 10)],
        )
        return carry

    lax.fori_loop(0, ROWS, cluster, 0)

    @pl.when(group == 0)
    def _():
        for c in output_copies():
            c.wait()

    rows = pl.ds(pl.multiple_of(group * WIDE, WIDE), WIDE)
    part = jnp.dot(
        ctx[...].reshape(ROWS * CS, WIDE), weight[rows], preferred_element_type=F32
    )

    @pl.when(group == 0)
    def _():
        acc[...] = part

    @pl.when(jnp.logical_and(group > 0, group < groups - 1))
    def _():
        acc[...] += part

    @pl.when(group == groups - 1)
    def _():
        o_ref[...] = (f_ref[...].astype(F32) + acc[...] + part).astype(BF)


def attend(slots, counts, starts, queries, keys, values, squares, features, shard, arrays):
    hbm = pl.BlockSpec(memory_space=pltpu.HBM)
    window = (D // WIDE, 3 * ROWS, CS, WIDE)
    return pl.pallas_call(
        attend_kernel,
        out_shape=jax.ShapeDtypeStruct((ROWS * CS, D), BF),
        grid_spec=pltpu.PrefetchScalarGridSpec(
            num_scalar_prefetch=3,
            grid=(D // WIDE,),
            in_specs=[
                pl.BlockSpec((ROWS, CS, WIDE), lambda g, *_: (0, 0, g)),
                pl.BlockSpec((ROWS * CS, D), lambda g, *_: (0, 0)),
            ]
            + [pl.BlockSpec((8, 128), lambda g, *_: (0, 0))] * 4
            + [hbm] * (6 + 7),
            out_specs=pl.BlockSpec((ROWS * CS, D), lambda g, *_: (0, 0)),
            scratch_shapes=[
                pltpu.VMEM(window, BF),
                pltpu.VMEM(window, BF),
                pltpu.VMEM((ROWS, CS, WIDE), BF),
                pltpu.VMEM((ROWS * CS, D), F32),
                pltpu.VMEM((D, D), BF),
                pltpu.SemaphoreType.DMA((PIECES,)),
                pltpu.SemaphoreType.DMA((D // WIDE, 6)),
            ],
        ),
        compiler_params=pltpu.CompilerParams(vmem_limit_bytes=60 << 20),
        cost_estimate=pl.CostEstimate(
            flops=30 << 30, bytes_accessed=20 << 20, transcendentals=0
        ),
        name="attend",
    )(slots, counts, starts, queries, features, *squares, *keys, *values, shard, *arrays)


def key_slots(adjacency, valid, node, core):
    row = adjacency[:, 0, :] - node * ROWS
    low = jnp.where(core == 0, 3 * ROWS, 2 * ROWS)
    high = jnp.where(core == 0, 0, ROWS)
    index = row + jnp.where(row < 0, low, jnp.where(row >= ROWS, high, 0))
    used = (valid[:, 0, :] > 0).astype(jnp.int32)
    before = jnp.sum(
        used[:, None, :] * (jnp.arange(8)[None, :, None] > jnp.arange(8)[None, None, :]), -1
    )
    hit = used[:, :, None] * (before[:, :, None] == jnp.arange(8)[None, None, :])
    listed = jnp.sum(index[:, :, None] * hit, 1)
    own = jnp.arange(ROWS, dtype=jnp.int32)[:, None]
    return jnp.concatenate([own, listed], 1).astype(jnp.int32), (
        1 + jnp.sum(used, 1)
    ).astype(jnp.int32)


def per_device(
    features, norm_gain, query_weight, key_weight, value_weight, output_weight, adjacency, valid
):
    flat = features.reshape(ROWS * CS, D)
    n = lax.axis_size("z") * lax.axis_size("x") * 2
    pairs = [(i, i + 1) for i in range(1, n - 1, 2)]
    off = lax.ppermute(flat, NODES, pairs + [(j, i) for i, j in pairs])
    core = lax.axis_index("core")
    shards = (key_weight, value_weight, query_weight)
    part, output_part = split_rows(shards + (output_weight,), core)
    tables = (
        *key_slots(adjacency, valid, lax.axis_index(NODES), core),
        place_starts(lax.axis_index("fsdp"), core),
    )
    arrays, (slots, counts, starts) = relayed_rows(part, tables)
    output_part, _ = lax.optimization_barrier((output_part, arrays[2:4]))
    output_arrays = direct_rows(output_part)
    gain = norm_gain.reshape(1, D)
    mine, off = lax.optimization_barrier((flat, off))
    keys, values, queries, own_squares, query_squares = project(
        "own", mine, gain, starts, shards, arrays, 3, (1.0, 1.0, QSCALE), (0, 2)
    )
    near_keys, near_values = swap_cores(keys), swap_cores(values)
    near_squares = swap_cores(own_squares)
    queries, *output_arrays = lax.optimization_barrier((queries, *output_arrays))
    output_arrays += [swap_cores(t) for t in output_arrays]
    off_keys, off_values, off_squares = project(
        "off", off, gain, starts, shards[:2], arrays, 3, (1.0, 1.0), (0,)
    )

    def cells(t):
        return t.reshape(ROWS, CS, D)

    out = attend(
        slots,
        counts,
        starts,
        cells(queries),
        [cells(t) for t in (keys, near_keys, off_keys)],
        [cells(t) for t in (values, near_values, off_values)],
        (own_squares, near_squares, off_squares, query_squares),
        mine,
        output_weight,
        output_arrays,
    )
    return out.reshape(ROWS, 1, CS, D)


def solution(mesh):
    nodes, fsdp = mesh.devices.shape
    split = Mesh(mesh.devices.reshape(nodes // 8, 4, 2, fsdp), NODES + ("fsdp",))
    in_specs = (
        P(NODES, "fsdp", None, None),
        P(),
        P("fsdp", None),
        P("fsdp", None),
        P("fsdp", None),
        P("fsdp", None),
        P(NODES, "fsdp", None),
        P(NODES, "fsdp", None),
    )
    out_specs = P(NODES, "fsdp", None, None)
    return jax.shard_map(
        per_device, mesh=split, in_specs=in_specs, out_specs=out_specs, check_vma=False
    )
```

```python
import functools

import jax
import jax.numpy as jnp
from jax import lax
from jax.experimental import pallas as pl
from jax.experimental.pallas import tpu as pltpu
from jax.sharding import Mesh
from jax.sharding import PartitionSpec as P

BF = jnp.bfloat16
F32 = jnp.float32
NODES = ("z", "x", "core")
HSIZE = 64
QSCALE = 1.4426950408889634 / HSIZE**0.5
ROWS = 8
CS = 128
D = 1024
TILE = 512
SHARD = 256
WIDE = 512
SAFE = 9000.0


def swap_cores(t):
    return lax.ppermute(t, "core", [(0, 1), (1, 0)])


def split_kernel(core, k_ref, v_ref, q_ref, o_ref, first, second):
    half = SHARD // 2
    for i, ref in enumerate((k_ref, v_ref, q_ref)):
        first[i * half : (i + 1) * half] = ref[...]
    second[...] = o_ref[...]


def split_rows(weights, core):
    half = SHARD // 2
    return pl.pallas_call(
        split_kernel,
        out_shape=[
            jax.ShapeDtypeStruct((3 * half, D), BF),
            jax.ShapeDtypeStruct((half, D), BF),
        ],
        grid_spec=pltpu.PrefetchScalarGridSpec(
            num_scalar_prefetch=1,
            grid=(1,),
            in_specs=[pl.BlockSpec((half, D), lambda i, c: (c[0], 0))] * 4,
            out_specs=[
                pl.BlockSpec((3 * half, D), lambda i, c: (0, 0)),
                pl.BlockSpec((half, D), lambda i, c: (0, 0)),
            ],
        ),
        name="split_rows",
    )(core.reshape(1), *weights)


UP = [(i, (i + 1) % 4) for i in range(4)]
DOWN = [((i + 1) % 4, i) for i in range(4)]


def relayed_rows(part, after):
    half = part.shape[0] // 2
    below = lax.ppermute(part, "fsdp", UP)
    above = lax.ppermute(part, "fsdp", DOWN)
    below, above, after = lax.optimization_barrier((below, above, after))
    far = (
        lax.ppermute(below[:half], "fsdp", UP),
        lax.ppermute(above[half:], "fsdp", DOWN),
    )
    mine = (below, above) + far
    return mine + tuple(swap_cores(t) for t in mine), after


def direct_rows(part):
    return [
        lax.ppermute(part, "fsdp", [(i, (i + k) % 4) for i in range(4)]) for k in (1, 3, 2)
    ]


def piece_plan(index, count):
    h = SHARD // 2
    if count == 1:
        return [(i, 0, h, i + 1, 0) for i in range(6)]
    total = count * h
    plan = []
    for side in range(2):
        plan.append((4 * side, index * h, h, 1 + 3 * side, 0))
        plan.append((4 * side + 1, index * h, h, 2 + 3 * side, 0))
        for part, (lo, hi) in enumerate(((0, total // 2), (total // 2, total))):
            first = max(lo, index * h)
            last = min(hi, (index + 1) * h)
            if first < last:
                plan.append(
                    (4 * side + 2 + part, first - lo, last - first, 3 + 3 * side, first - index * h)
                )
    return plan


def place_starts(y, core):
    h = SHARD // 2
    starts = [y * SHARD]
    for side in (core, 1 - core):
        starts += [(y + k) % 4 * SHARD + side * h for k in (3, 1, 2)]
    return jnp.stack(starts).astype(jnp.int32)


def weight_copies(starts, shard, arrays, index, count, target, sems):
    row = pl.multiple_of(starts[0], SHARD)
    copies = [pltpu.make_async_copy(shard, target.at[pl.ds(row, SHARD)], sems.at[0])]
    for n, (array, first, rows, place, offset) in enumerate(piece_plan(index, count)):
        row = pl.multiple_of(starts[place] + offset, 64)
        copies.append(
            pltpu.make_async_copy(
                arrays[array].at[pl.ds(first, rows)],
                target.at[pl.ds(row, rows)],
                sems.at[n + 1],
            )
        )
    return copies


PIECES = 9


def head_squares(t):
    wide = D // 2
    squares = t[:, :wide] * t[:, :wide] + t[:, wide:] * t[:, wide:]
    lane = lax.broadcasted_iota(jnp.int32, (wide, 128), 1)
    feature = lax.broadcasted_iota(jnp.int32, (wide, 128), 0)
    pick = (feature // HSIZE == lane).astype(BF)
    sums = jnp.dot(squares.astype(BF), pick, preferred_element_type=F32)
    return jnp.broadcast_to(jnp.max(sums, axis=0, keepdims=True), (8, 128))


def project_kernel(starts, x_ref, gain_ref, *refs, count, stacked, scales, squared):
    shards, arrays, refs = refs[:count], refs[count : count + 8], refs[count + 8 :]
    outs, squares, (weights, sems) = refs[:count], refs[count:-2], refs[-2:]
    step = pl.program_id(0)

    def copies(w):
        return weight_copies(starts, shards[w], arrays, w, stacked, weights.at[w], sems.at[w])

    @pl.when(step == 0)
    def _():
        for w in range(count):
            for c in copies(w):
                c.start()
        for ref in squares:
            ref[...] = jnp.zeros_like(ref)

    wide = x_ref[...].astype(F32)
    mean = jnp.mean(wide * wide, axis=-1, keepdims=True)
    normed = (wide * lax.rsqrt(mean + 1e-06) * gain_ref[...]).astype(BF)
    for w in range(count):

        @pl.when(step == 0)
        def _():
            for c in copies(w):
                c.wait()

        got = jnp.dot(normed, weights[w], preferred_element_type=F32)
        if scales[w] != 1.0:
            got = got * scales[w]
        if w in squared:
            ref = squares[squared.index(w)]
            ref[...] = jnp.maximum(ref[...], head_squares(got))
        outs[w][...] = got.astype(BF)


def project(name, x, gain, starts, shards, arrays, stacked, scales, squared):
    count = len(shards)
    rows = x.shape[0]
    return pl.pallas_call(
        functools.partial(
            project_kernel, count=count, stacked=stacked, scales=scales, squared=squared
        ),
        out_shape=[jax.ShapeDtypeStruct((rows, D), BF)] * count
        + [jax.ShapeDtypeStruct((8, 128), F32)] * len(squared),
        grid_spec=pltpu.PrefetchScalarGridSpec(
            num_scalar_prefetch=1,
            grid=(rows // TILE,),
            in_specs=[
                pl.BlockSpec((TILE, D), lambda i, s: (i, 0)),
                pl.BlockSpec((1, D), lambda i, s: (0, 0)),
            ]
            + [pl.BlockSpec(memory_space=pltpu.HBM)] * (count + 8),
            out_specs=[pl.BlockSpec((TILE, D), lambda i, s: (i, 0))] * count
            + [pl.BlockSpec((8, 128), lambda i, s: (0, 0))] * len(squared),
            scratch_shapes=[
                pltpu.VMEM((count, D, D), BF),
                pltpu.SemaphoreType.DMA((count, PIECES)),
            ],
        ),
        compiler_params=pltpu.CompilerParams(vmem_limit_bytes=56 << 20),
        cost_estimate=pl.CostEstimate(
            flops=2 * rows * D * D * count * 16,
            bytes_accessed=2 * (rows * D * (1 + count) + count * D * D),
            transcendentals=0,
        ),
        name=name,
    )(starts, x, gain, *shards, *arrays)


def attend_kernel(slots, counts, starts, q_ref, f_ref, *refs):
    square_refs, refs = refs[:4], refs[4:]
    key_refs, value_refs, refs = refs[:3], refs[3:6], refs[6:]
    shard, arrays, refs = refs[0], refs[1:7], refs[7:]
    o_ref, keys, values, ctx, acc, weight, wide, weight_sems, sems, wide_sem = refs
    residual = pltpu.make_async_copy(f_ref, wide, wide_sem)
    group = pl.program_id(0)
    groups = pl.num_programs(0)

    def output_copies():
        return weight_copies(starts, shard, arrays, 0, 1, weight, weight_sems)

    def window_copies(g):
        lanes = pl.ds(pl.multiple_of(g * WIDE, WIDE), WIDE)
        for n, (sources, target) in enumerate(((key_refs, keys), (value_refs, values))):
            for p in range(3):
                yield pltpu.make_async_copy(
                    sources[p].at[:, :, lanes],
                    target.at[g, pl.ds(p * ROWS, ROWS)],
                    sems.at[g, 3 * n + p],
                )

    @pl.when(group == 0)
    def _():
        for g in range(D // WIDE):
            for c in window_copies(g):
                c.start()
        for c in output_copies():
            c.start()
        residual.start()

    for c in window_copies(group):
        c.wait()

    key_squares = jnp.maximum(
        jnp.maximum(square_refs[0][...], square_refs[1][...]), square_refs[2][...]
    )
    shifted = jnp.where(jnp.max(key_squares * square_refs[3][...]) < SAFE, 0, 9)

    def cluster(r, carry):
        def variant(blocks, shift):
            def run():
                head = lax.broadcasted_iota(jnp.int32, (CS, 128), 1) // HSIZE
                left = head == 0
                ids = [slots[r, j] for j in range(blocks)]
                for t in range(WIDE // 128):
                    lanes = slice(128 * t, 128 * t + 128)
                    q = q_ref[r, :, lanes]
                    stacked = jnp.concatenate(
                        [jnp.where(head == h, q, jnp.zeros_like(q)) for h in range(2)], 0
                    )
                    scores = []
                    for j in range(0, blocks, 2):
                        block = jnp.concatenate(
                            [keys[group, i, :, lanes] for i in ids[j : j + 2]], 0
                        )
                        scores.append(
                            lax.dot_general(
                                stacked,
                                block,
                                (((1,), (1,)), ((), ())),
                                preferred_element_type=F32,
                            )
                        )
                    if shift:
                        top = None
                        for s in scores:
                            for u in range(0, s.shape[1], 128):
                                part = s[:, u : u + 128]
                                top = part if top is None else jnp.maximum(top, part)
                        top = jnp.max(top, axis=1, keepdims=True)
                        scores = [s - top for s in scores]
                    total = None
                    for n, j in enumerate(range(0, blocks, 2)):
                        probs = jnp.exp2(scores[n]).astype(BF)
                        vals = jnp.concatenate(
                            [values[group, i, :, lanes] for i in ids[j : j + 2]], 0
                        )
                        both = jnp.concatenate([vals, jnp.ones(vals.shape, BF)], 1)
                        d = jnp.dot(probs, both, preferred_element_type=F32)
                        total = d if total is None else total + d
                    num = jnp.where(left, total[:CS, :128], total[CS:, :128])
                    den = jnp.where(left, total[:CS, 128:], total[CS:, 128:])
                    ctx[r, :, lanes] = (num / den).astype(BF)

            return run

        lax.switch(
            counts[r] - 1 + shifted,
            [variant(n, shift) for shift in (False, True) for n in range(1, 10)],
        )
        return carry

    lax.fori_loop(0, ROWS, cluster, 0)

    @pl.when(group == 0)
    def _():
        for c in output_copies():
            c.wait()

    rows = pl.ds(pl.multiple_of(group * WIDE, WIDE), WIDE)
    part = jnp.dot(
        ctx[...].reshape(ROWS * CS, WIDE), weight[rows], preferred_element_type=F32
    )

    @pl.when(group == 0)
    def _():
        acc[...] = part

    @pl.when(jnp.logical_and(group > 0, group < groups - 1))
    def _():
        acc[...] += part

    @pl.when(group == groups - 1)
    def _():
        residual.wait()
        o_ref[...] = (wide[...].astype(F32) + acc[...] + part).astype(BF)


def attend(slots, counts, starts, queries, keys, values, squares, features, shard, arrays):
    hbm = pl.BlockSpec(memory_space=pltpu.HBM)
    window = (D // WIDE, 3 * ROWS, CS, WIDE)
    return pl.pallas_call(
        attend_kernel,
        out_shape=jax.ShapeDtypeStruct((ROWS * CS, D), BF),
        grid_spec=pltpu.PrefetchScalarGridSpec(
            num_scalar_prefetch=3,
            grid=(D // WIDE,),
            in_specs=[
                pl.BlockSpec((ROWS, CS, WIDE), lambda g, *_: (0, 0, g)),
                hbm,
            ]
            + [pl.BlockSpec((8, 128), lambda g, *_: (0, 0))] * 4
            + [hbm] * (6 + 7),
            out_specs=pl.BlockSpec((ROWS * CS, D), lambda g, *_: (0, 0)),
            scratch_shapes=[
                pltpu.VMEM(window, BF),
                pltpu.VMEM(window, BF),
                pltpu.VMEM((ROWS, CS, WIDE), BF),
                pltpu.VMEM((ROWS * CS, D), F32),
                pltpu.VMEM((D, D), BF),
                pltpu.VMEM((ROWS * CS, D), BF),
                pltpu.SemaphoreType.DMA((PIECES,)),
                pltpu.SemaphoreType.DMA((D // WIDE, 6)),
                pltpu.SemaphoreType.DMA,
            ],
        ),
        compiler_params=pltpu.CompilerParams(vmem_limit_bytes=60 << 20),
        cost_estimate=pl.CostEstimate(
            flops=30 << 30, bytes_accessed=20 << 20, transcendentals=0
        ),
        name="attend",
    )(slots, counts, starts, queries, features, *squares, *keys, *values, shard, *arrays)


def key_slots(adjacency, valid, node, core):
    row = adjacency[:, 0, :] - node * ROWS
    low = jnp.where(core == 0, 3 * ROWS, 2 * ROWS)
    high = jnp.where(core == 0, 0, ROWS)
    index = row + jnp.where(row < 0, low, jnp.where(row >= ROWS, high, 0))
    used = (valid[:, 0, :] > 0).astype(jnp.int32)
    before = jnp.sum(
        used[:, None, :] * (jnp.arange(8)[None, :, None] > jnp.arange(8)[None, None, :]), -1
    )
    hit = used[:, :, None] * (before[:, :, None] == jnp.arange(8)[None, None, :])
    listed = jnp.sum(index[:, :, None] * hit, 1)
    own = jnp.arange(ROWS, dtype=jnp.int32)[:, None]
    return jnp.concatenate([own, listed], 1).astype(jnp.int32), (
        1 + jnp.sum(used, 1)
    ).astype(jnp.int32)


def per_device(
    features, norm_gain, query_weight, key_weight, value_weight, output_weight, adjacency, valid
):
    flat = features.reshape(ROWS * CS, D)
    n = lax.axis_size("z") * lax.axis_size("x") * 2
    pairs = [(i, i + 1) for i in range(1, n - 1, 2)]
    off = lax.ppermute(flat, NODES, pairs + [(j, i) for i, j in pairs])
    core = lax.axis_index("core")
    shards = (key_weight, value_weight, query_weight)
    part, output_part = split_rows(shards + (output_weight,), core)
    tables = (
        *key_slots(adjacency, valid, lax.axis_index(NODES), core),
        place_starts(lax.axis_index("fsdp"), core),
    )
    arrays, (slots, counts, starts) = relayed_rows(part, tables)
    output_part, _ = lax.optimization_barrier((output_part, arrays[2:4]))
    output_arrays = direct_rows(output_part)
    gain = norm_gain.reshape(1, D)
    mine, off = lax.optimization_barrier((flat, off))
    keys, values, queries, own_squares, query_squares = project(
        "own", mine, gain, starts, shards, arrays, 3, (1.0, 1.0, QSCALE), (0, 2)
    )
    near_keys, near_values = swap_cores(keys), swap_cores(values)
    near_squares = swap_cores(own_squares)
    queries, *output_arrays = lax.optimization_barrier((queries, *output_arrays))
    output_arrays += [swap_cores(t) for t in output_arrays]
    off_keys, off_values, off_squares = project(
        "off", off, gain, starts, shards[:2], arrays, 3, (1.0, 1.0), (0,)
    )

    def cells(t):
        return t.reshape(ROWS, CS, D)

    out = attend(
        slots,
        counts,
        starts,
        cells(queries),
        [cells(t) for t in (keys, near_keys, off_keys)],
        [cells(t) for t in (values, near_values, off_values)],
        (own_squares, near_squares, off_squares, query_squares),
        mine,
        output_weight,
        output_arrays,
    )
    return out.reshape(ROWS, 1, CS, D)


def solution(mesh):
    nodes, fsdp = mesh.devices.shape
    split = Mesh(mesh.devices.reshape(nodes // 8, 4, 2, fsdp), NODES + ("fsdp",))
    in_specs = (
        P(NODES, "fsdp", None, None),
        P(),
        P("fsdp", None),
        P("fsdp", None),
        P("fsdp", None),
        P("fsdp", None),
        P(NODES, "fsdp", None),
        P(NODES, "fsdp", None),
    )
    out_specs = P(NODES, "fsdp", None, None)
    return jax.shard_map(
        per_device, mesh=split, in_specs=in_specs, out_specs=out_specs, check_vma=False
    )
```
